512 devices in a mesh: dp: 8 (over y), row: 4 (over z_lo), col: 16 (over x, z_hi, core).
Axes of the slice: x: 4, y: 8, z: 8 (z_hi: 2, z_lo: 4; z = z_hi * 4 + z_lo), core: 2. Of those that a mesh axis runs over, the one named last changes fastest.
Arguments:
- tokens: bfloat16 [2048, 4096], P(('dp', 'col'), 'row'), may hold values from -6 to 6
- gate_weight: bfloat16 [4096, 14336], P('row', 'col'), may hold values from -0.125 to 0.125
- up_weight: bfloat16 [4096, 14336], P('row', 'col'), may hold values from -0.125 to 0.125
- gate_mask: int32 [32, 112], P('row', 'col'), may hold values 0 or 1
- up_mask: int32 [32, 112], P('row', 'col'), may hold values 0 or 1
- slope: bfloat16 [2048, 14336], P(('dp', 'row'), 'col'), may hold values from -6 to 6
Outputs:
- hidden: bfloat16 [2048, 14336], P(('dp', 'row'), 'col')
- input_grad: bfloat16 [2048, 4096], P(('dp', 'col'), 'row')
- gate_grad: bfloat16 [32, 128, 14336], P('row', 'dp', 'col')
- up_grad: bfloat16 [32, 128, 14336], P('row', 'dp', 'col')
The draws below stay inside these ranges and needn't reach their ends.
Inputs may be any that keep to these rules, and one draw needn't show every extreme that they name: `gate_mask`: 1 marks a live 128 x 128 block of the projection, 0 a pruned one. `up_mask`: 1 marks a live 128 x 128 block of the projection, 0 a pruned one.
All inputs are finite; a program needn't handle non-finite values.
Results may differ from the reference program's by a relative error of at most 0.0058.
Values may be sent and summed in bfloat16 or wider, within the bound.
No kernel may reach another device: no remote copies, remote signals or barrier semaphores. Data moves between devices by JAX's collectives and lax.ppermute only.
A program may use at most 64 MiB of HBM per device.

```python
import jax
import jax.numpy as jnp
from jax import lax

D = 4096
FF = 14336
BLOCK = 128
TOK = 256
TOKENS = 2048
N_DP = 8


def place_ends(drawn, own_key, least, largest):
    place = [jax.random.randint(jax.random.fold_in(own_key, axis), (), 0, length) for axis, length in enumerate(drawn.shape)]
    widest = drawn.shape.index(max(drawn.shape))
    neighbour = place[:widest] + [(place[widest] + 1) % drawn.shape[widest]] + place[widest + 1:]
    return drawn.at[tuple(place)].set(least).at[tuple(neighbour)].set(largest)


def block_levels(stream_key, extent, cuts, least, largest):
    factor_of, own = 1.0, jax.random.fold_in(stream_key, 6)
    for position, blocks in cuts:
        heights = jnp.exp(jax.random.uniform(jax.random.fold_in(own, position), (blocks,), jnp.float32, least / len(cuts), largest / len(cuts)))
        factor_of = factor_of * jnp.repeat(heights, extent[position] // blocks).reshape([-1 if axis == position else 1 for axis in range(len(extent))])
    return factor_of


def centred(rng, shape, scale, most, shards=(), kind=jnp.bfloat16):
    loudness = block_levels(rng, shape, shards, -0.22, 0.18) if shards else 1.0
    drawn = jax.random.normal(rng, shape, jnp.float32) * scale * loudness
    return jnp.minimum(jnp.maximum(drawn, -most), most).astype(kind)


def setup_inputs(seed: int = 0) -> dict:
    key_of = jax.random.split(jax.random.key(seed), 7)
    return {
        "tokens": centred(key_of[0], (TOKENS, D), 1.0, 6.0, ((0, 128), (1, 4))),
        "gate_weight": centred(key_of[1], (D, FF), (D // 2) ** -0.5, 0.125, ((0, 4), (1, 16))),
        "up_weight": centred(key_of[2], (D, FF), (D // 2) ** -0.5, 0.125, ((0, 4), (1, 16))),
        "gate_mask": place_ends((jax.random.randint(key_of[3], (D // BLOCK, FF // BLOCK), 0, 2) < 1).astype(jnp.int32), jax.random.fold_in(key_of[3], 1), 0, 1),
        "up_mask": place_ends((jax.random.randint(key_of[4], (D // BLOCK, FF // BLOCK), 0, 2) < 1).astype(jnp.int32), jax.random.fold_in(key_of[4], 1), 0, 1),
        "slope": centred(key_of[5], (TOKENS, FF), 1.0, 6.0, ((0, 32), (1, 16))),
    }


def spread(mask):
    grid = mask.astype(jnp.float32)
    return jnp.repeat(jnp.repeat(grid, BLOCK, axis=0), BLOCK, axis=1)


def reference(tokens, gate_weight, up_weight, gate_mask, up_mask, slope):
    gate_spread = spread(gate_mask)
    up_spread = spread(up_mask)
    gate_live = (gate_weight.astype(jnp.float32) * gate_spread).astype(jnp.bfloat16)
    up_live = (up_weight.astype(jnp.float32) * up_spread).astype(jnp.bfloat16)
    paired = jnp.concatenate([gate_live, up_live], axis=1)
    sums = jnp.dot(tokens, paired, preferred_element_type=jnp.float32)
    gate = sums[:, :FF]
    up = sums[:, FF:]
    sigma = jax.nn.sigmoid(gate)
    act = gate * sigma
    hidden = (act * up).astype(jnp.bfloat16)
    slope_wide = slope.astype(jnp.float32)
    gate_slope = (slope_wide * up * sigma * (1.0 + gate * (1.0 - sigma))).astype(jnp.bfloat16)
    up_slope = (slope_wide * act).astype(jnp.bfloat16)
    slopes = jnp.concatenate([gate_slope, up_slope], axis=1)
    input_grad = lax.dot_general(slopes, paired, (((1,), (1,)), ((), ())), preferred_element_type=jnp.float32).astype(jnp.bfloat16)

    def add_replica(carry, index):
        start = (index * TOK).astype(jnp.int32)
        feats = lax.dynamic_slice_in_dim(tokens, start, TOK, 0)
        parts = lax.dynamic_slice_in_dim(slopes, start, TOK, 0)
        term = lax.dot_general(feats, parts, (((0,), (0,)), ((), ())), preferred_element_type=jnp.float32).astype(jnp.bfloat16)
        term = lax.optimization_barrier(term)
        return carry + term.astype(jnp.float32), None

    total, unused = lax.scan(add_replica, jnp.zeros((D, 2 * FF), jnp.float32), jnp.arange(N_DP, dtype=jnp.int32))
    gate_grad = (total[:, :FF] * gate_spread).astype(jnp.bfloat16).reshape(D // BLOCK, BLOCK, FF)
    up_grad = (total[:, FF:] * up_spread).astype(jnp.bfloat16).reshape(D // BLOCK, BLOCK, FF)
    return hidden, input_grad, gate_grad, up_grad
```

```python
import jax
import jax.numpy as jnp
from jax import lax
from jax.experimental import pallas as pl
from jax.experimental.pallas import tpu as pltpu
from jax.sharding import PartitionSpec as P

BF = jnp.bfloat16
F32 = jnp.float32
FIRST_SHARE = 4


def masked_pair(gate_w, up_w, gate_mask, up_mask, block, column):
    rows = gate_w.shape[0] // block
    pieces = []
    for b in range(rows):
        part = pl.ds(b * block, block)
        g = gate_w[part, :].astype(F32) * gate_mask[b, column].astype(F32)
        u = up_w[part, :].astype(F32) * up_mask[b, column].astype(F32)
        pieces.append(jnp.concatenate([g, u], axis=1).astype(BF))
    return jnp.concatenate(pieces, axis=0)


def forward(tokens, gate_weight, up_weight, gate_mask, up_mask, first, count):
    block = gate_weight.shape[0] // gate_mask.shape[0]
    toks, depth = tokens.shape

    def kernel(gm, um, t, gw, uw, out):
        pair = masked_pair(gw, uw, gm, um, block, pl.program_id(0) + first)
        out[...] = jnp.dot(t[...], pair, preferred_element_type=F32).astype(BF)

    smem = pl.BlockSpec(memory_space=pltpu.SMEM)
    return pl.pallas_call(
        kernel,
        grid=(count,),
        in_specs=[
            smem,
            smem,
            pl.BlockSpec((toks, depth), lambda j: (0, 0)),
            pl.BlockSpec((depth, block), lambda j: (0, j + first)),
            pl.BlockSpec((depth, block), lambda j: (0, j + first)),
        ],
        out_specs=pl.BlockSpec((toks, 2 * block), lambda j: (0, j)),
        out_shape=jax.ShapeDtypeStruct((toks, count * 2 * block), BF),
        cost_estimate=pl.CostEstimate(
            flops=4 * toks * depth * count * block,
            bytes_accessed=4 * depth * count * block + 2 * toks * depth,
            transcendentals=0,
        ),
        name="forward",
    )(gate_mask, up_mask, tokens, gate_weight, up_weight)


def activate(received, slope, block, first, count, replicas_of_sum, hidden_before):
    here = slope.shape[0]

    def kernel(*refs):
        r, s = refs[0], refs[1]
        hidden, slopes = refs[-2], refs[-1]
        total = r[pl.ds(0, here), :].astype(F32)
        for k in range(1, replicas_of_sum):
            total = total + r[pl.ds(k * here, here), :].astype(F32)
        gate, up = total[:, :block], total[:, block:]
        sigma = jax.nn.sigmoid(gate)
        act = gate * sigma
        hidden[...] = (act * up).astype(BF)
        wide = s[...].astype(F32)
        gate_slope = (wide * up * sigma * (1.0 + gate * (1.0 - sigma))).astype(BF)
        slopes[...] = jnp.concatenate([gate_slope, (wide * act).astype(BF)], axis=1)

    in_specs = [
        pl.BlockSpec((here * replicas_of_sum, 2 * block), lambda j: (0, j)),
        pl.BlockSpec((here, block), lambda j: (0, j + first)),
    ]
    operands = [received, slope]
    aliases = {}
    if hidden_before is not None:
        in_specs.append(pl.BlockSpec(memory_space=pl.ANY))
        operands.append(hidden_before)
        aliases = {2: 0}
    return pl.pallas_call(
        kernel,
        grid=(count,),
        in_specs=in_specs,
        out_specs=[
            pl.BlockSpec((here, block), lambda j: (0, j + first)),
            pl.BlockSpec((here, 2 * block), lambda j: (0, j)),
        ],
        out_shape=[
            jax.ShapeDtypeStruct(slope.shape, BF),
            jax.ShapeDtypeStruct((here, count * 2 * block), BF),
        ],
        input_output_aliases=aliases,
        cost_estimate=pl.CostEstimate(
            flops=30 * here * count * block,
            bytes_accessed=here * count * block * 24,
            transcendentals=here * count * block,
        ),
        name="activate",
    )(*operands)


def parts_of(tokens, slopes, block, replicas, count):
    toks, depth = tokens.shape
    share = block // replicas
    blocks_down = depth // block

    def kernel(t, s, out, flipped):
        @pl.when(pl.program_id(0) == 0)
        def _():
            turned = t[...].T
            for b in range(blocks_down):
                for d in range(replicas):
                    flipped[pl.ds((d * blocks_down + b) * share, share), :] = turned[
                        b * block + d * share : b * block + (d + 1) * share, :
                    ]

        out[...] = jnp.dot(flipped[...], s[...], preferred_element_type=F32).astype(BF)

    return pl.pallas_call(
        kernel,
        grid=(count,),
        in_specs=[
            pl.BlockSpec((toks, depth), lambda j: (0, 0)),
            pl.BlockSpec((toks, 2 * block), lambda j: (0, j)),
        ],
        out_specs=pl.BlockSpec((depth, 2 * block), lambda j: (0, j)),
        out_shape=jax.ShapeDtypeStruct((depth, count * 2 * block), BF),
        scratch_shapes=[pltpu.VMEM((depth, toks), BF)],
        cost_estimate=pl.CostEstimate(
            flops=4 * toks * depth * count * block,
            bytes_accessed=4 * depth * count * block + 2 * toks * depth,
            transcendentals=0,
        ),
        name="parts",
    )(tokens, slopes)


def backward(slopes, gate_weight, up_weight, gate_mask, up_mask, counts):
    block = gate_weight.shape[0] // gate_mask.shape[0]
    depth = gate_weight.shape[0]
    toks = slopes[0].shape[0]
    total = sum(counts)
    starts = [sum(counts[:i]) for i in range(len(counts))]

    def kernel(gm, um, *refs):
        gw, uw, out = refs[-3], refs[-2], refs[-1]
        j = pl.program_id(0)
        pair = masked_pair(gw, uw, gm, um, block, j)

        @pl.when(j == 0)
        def _():
            out[...] = jnp.zeros_like(out)

        for start, count, s in zip(starts, counts, refs[: len(counts)]):

            @pl.when((j >= start) & (j < start + count))
            def _(s=s):
                out[...] += lax.dot_general(
                    s[...], pair, (((1,), (1,)), ((), ())), preferred_element_type=F32
                )

    def piece(start, count):
        return pl.BlockSpec(
            (toks, 2 * block), lambda j: (0, jnp.minimum(jnp.maximum(j - start, 0), count - 1))
        )

    smem = pl.BlockSpec(memory_space=pltpu.SMEM)
    return pl.pallas_call(
        kernel,
        grid=(total,),
        in_specs=[smem, smem]
        + [piece(start, count) for start, count in zip(starts, counts)]
        + [
            pl.BlockSpec((depth, block), lambda j: (0, j)),
            pl.BlockSpec((depth, block), lambda j: (0, j)),
        ],
        out_specs=pl.BlockSpec((toks, depth), lambda j: (0, 0)),
        out_shape=jax.ShapeDtypeStruct((toks, depth), F32),
        cost_estimate=pl.CostEstimate(
            flops=4 * toks * depth * total * block,
            bytes_accessed=4 * depth * total * block + 4 * toks * depth,
            transcendentals=0,
        ),
        name="backward",
    )(gate_mask, up_mask, *slopes, gate_weight, up_weight)


def finish(sums, gate_mask, up_mask, block, counts):
    rows = sums[0].shape[0]
    blocks_down = gate_mask.shape[0]
    share = rows // blocks_down
    total = sum(counts)

    def kernel(gm, um, *refs):
        gate_out, up_out = refs[-2], refs[-1]
        at = 0
        for count, s in zip(counts, refs):
            for c in range(count):
                columns = pl.ds(at * block, block)
                for b in range(blocks_down):
                    part = pl.ds(b * share, share)
                    g = s[part, pl.ds(2 * c * block, block)].astype(F32)
                    u = s[part, pl.ds((2 * c + 1) * block, block)].astype(F32)
                    gate_out[b, :, columns] = (g * gm[b, at].astype(F32)).astype(BF)
                    up_out[b, :, columns] = (u * um[b, at].astype(F32)).astype(BF)
                at += 1

    smem = pl.BlockSpec(memory_space=pltpu.SMEM)
    vmem = pl.BlockSpec(memory_space=pltpu.VMEM)
    shape = jax.ShapeDtypeStruct((blocks_down, share, total * block), BF)
    return pl.pallas_call(
        kernel,
        in_specs=[smem, smem] + [vmem] * len(sums),
        out_specs=[vmem, vmem],
        out_shape=[shape, shape],
        name="finish",
    )(gate_mask, up_mask, *sums)


def body(tokens, gate_weight, up_weight, gate_mask, up_mask, slope):
    block = gate_weight.shape[0] // gate_mask.shape[0]
    total = gate_mask.shape[1]
    rows = lax.axis_size("row")
    replicas = lax.axis_size("dp")
    cols = lax.axis_size("col")
    counts = (FIRST_SHARE, total - FIRST_SHARE) if FIRST_SHARE else (total,)
    gathered = lax.all_gather(tokens, "col", axis=0, tiled=True)
    hidden = None
    all_slopes, sums = [], []
    first = 0
    for count in counts:
        partial = forward(gathered, gate_weight, up_weight, gate_mask, up_mask, first, count)
        received = lax.all_to_all(partial, "row", 0, 0, tiled=True)
        hidden, slopes = activate(received, slope, block, first, count, rows, hidden)
        slopes = lax.all_gather(slopes, "row", axis=0, tiled=True)
        parts = parts_of(gathered, slopes, block, replicas, count)
        sums.append(lax.psum_scatter(parts, "dp", scatter_dimension=0, tiled=True))
        all_slopes.append(slopes)
        first += count
    share = backward(all_slopes, gate_weight, up_weight, gate_mask, up_mask, counts)
    pieces = lax.all_to_all(share, "col", 0, 0, tiled=True)
    input_grad = jnp.sum(pieces.reshape((cols, -1) + pieces.shape[1:]), axis=0).astype(BF)
    gate_grad, up_grad = finish(sums, gate_mask, up_mask, block, counts)
    return hidden, input_grad, gate_grad, up_grad


def solution(mesh):
    return jax.shard_map(
        body,
        mesh=mesh,
        in_specs=(
            P(("dp", "col"), "row"),
            P("row", "col"),
            P("row", "col"),
            P("row", "col"),
            P("row", "col"),
            P(("dp", "row"), "col"),
        ),
        out_specs=(
            P(("dp", "row"), "col"),
            P(("dp", "col"), "row"),
            P("row", "dp", "col"),
            P("row", "dp", "col"),
        ),
        check_vma=False,
    )
```

```python
import jax
import jax.numpy as jnp
from jax import lax
from jax.experimental import pallas as pl
from jax.experimental.pallas import tpu as pltpu
from jax.sharding import PartitionSpec as P

BF = jnp.bfloat16
F32 = jnp.float32
MIB = 1024 * 1024
SPLIT = 4


def live_pair(gate_w, up_w, gate_mask, up_mask, block, column):
    rows = gate_w.shape[0] // block
    here = pl.ds(column * block, block)
    pieces = []
    for b in range(rows):
        part = pl.ds(b * block, block)
        g = gate_w[part, here] * gate_mask[b, column].astype(F32).astype(BF)
        u = up_w[part, here] * up_mask[b, column].astype(F32).astype(BF)
        pieces.append(jnp.concatenate([g, u], axis=1))
    return jnp.concatenate(pieces, axis=0)


def in_smem():
    return pl.BlockSpec(memory_space=pltpu.SMEM)


def in_vmem():
    return pl.BlockSpec(memory_space=pltpu.VMEM)


def forward(tokens, gate_weight, up_weight, gate_mask, up_mask):
    block = gate_weight.shape[0] // gate_mask.shape[0]
    toks, depth = tokens.shape
    count = gate_mask.shape[1]

    def kernel(gm, um, t, gw, uw, out, live):
        for j in range(count):
            live[:, pl.ds(2 * j * block, 2 * block)] = live_pair(gw, uw, gm, um, block, j)
        out[...] = jnp.dot(t[...], live[...], preferred_element_type=F32).astype(BF)

    return pl.pallas_call(
        kernel,
        in_specs=[in_smem(), in_smem(), in_vmem(), in_vmem(), in_vmem()],
        out_specs=[in_vmem(), in_vmem()],
        out_shape=[
            jax.ShapeDtypeStruct((toks, count * 2 * block), BF),
            jax.ShapeDtypeStruct((depth, count * 2 * block), BF),
        ],
        cost_estimate=pl.CostEstimate(
            flops=4 * toks * depth * count * block,
            bytes_accessed=8 * depth * count * block + 2 * toks * depth,
            transcendentals=0,
        ),
        compiler_params=pltpu.CompilerParams(vmem_limit_bytes=24 * MIB),
        name="forward",
    )(gate_mask, up_mask, tokens, gate_weight, up_weight)


def activate(received, slope, block, sources):
    here, width = slope.shape
    count = width // block

    def kernel(r, s, hidden, slopes):
        for j in range(count):
            both = pl.ds(2 * j * block, 2 * block)
            total = r[pl.ds(0, here), both].astype(F32)
            for k in range(1, sources):
                total = total + r[pl.ds(k * here, here), both].astype(F32)
            gate, up = total[:, :block], total[:, block:]
            sigma = jax.nn.sigmoid(gate)
            act = gate * sigma
            one = pl.ds(j * block, block)
            hidden[:, one] = (act * up).astype(BF)
            wide = s[:, one].astype(F32)
            gate_slope = (wide * up * sigma * (1.0 + gate * (1.0 - sigma))).astype(BF)
            slopes[:, both] = jnp.concatenate([gate_slope, (wide * act).astype(BF)], axis=1)

    return pl.pallas_call(
        kernel,
        in_specs=[in_vmem(), in_vmem()],
        out_specs=[in_vmem(), in_vmem()],
        out_shape=[
            jax.ShapeDtypeStruct((here, width), BF),
            jax.ShapeDtypeStruct((here, 2 * width), BF),
        ],
        cost_estimate=pl.CostEstimate(
            flops=30 * here * width,
            bytes_accessed=here * width * 24,
            transcendentals=here * width,
        ),
        compiler_params=pltpu.CompilerParams(vmem_limit_bytes=12 * MIB),
        name="activate",
    )(received, slope)


def parts_of(tokens, slopes, block, replicas, counts):
    toks, depth = tokens.shape
    share = block // replicas
    blocks_down = depth // block
    each = blocks_down * share
    widths = [2 * block * count for count in counts]
    steps = 4
    group = replicas // steps

    def kernel(t, s, *refs):
        flipped = refs[-1]
        step = pl.program_id(0)

        @pl.when(step == 0)
        def _():
            turned = t[...].T
            for b in range(blocks_down):
                for d in range(replicas):
                    flipped[pl.ds((d * blocks_down + b) * share, share), :] = turned[
                        b * block + d * share : b * block + (d + 1) * share, :
                    ]

        rows = flipped[pl.ds(pl.multiple_of(step * (group * each), group * each), group * each), :]
        at = 0
        for out, width in zip(refs, widths):
            part = jnp.dot(rows, s[:, pl.ds(at, width)], preferred_element_type=F32).astype(BF)
            for i in range(group):
                out[i] = part[i * each : (i + 1) * each, :]
            at += width

    return pl.pallas_call(
        kernel,
        grid=(steps,),
        in_specs=[in_vmem(), in_vmem()],
        out_specs=[pl.BlockSpec((group, each, width), lambda i: (i, 0, 0)) for width in widths],
        out_shape=[jax.ShapeDtypeStruct((replicas, each, width), BF) for width in widths],
        scratch_shapes=[pltpu.VMEM((depth, toks), BF)],
        cost_estimate=pl.CostEstimate(
            flops=2 * toks * depth * sum(widths),
            bytes_accessed=2 * depth * sum(widths) + 2 * toks * depth,
            transcendentals=0,
        ),
        compiler_params=pltpu.CompilerParams(vmem_limit_bytes=24 * MIB),
        name="parts",
    )(tokens, slopes)


def backward(slopes, live):
    toks, width = slopes.shape
    depth = live.shape[0]

    def kernel(s, w, out):
        out[...] = lax.dot_general(
            s[...], w[...], (((1,), (1,)), ((), ())), preferred_element_type=F32
        )

    return pl.pallas_call(
        kernel,
        in_specs=[in_vmem(), in_vmem()],
        out_specs=in_vmem(),
        out_shape=jax.ShapeDtypeStruct((toks, depth), F32),
        cost_estimate=pl.CostEstimate(
            flops=2 * toks * depth * width,
            bytes_accessed=2 * depth * width + 4 * toks * depth,
            transcendentals=0,
        ),
        compiler_params=pltpu.CompilerParams(vmem_limit_bytes=24 * MIB),
        name="backward",
    )(slopes, live)


def reduce_parts(chunks):
    replicas = lax.axis_size("dp")
    here = lax.axis_index("dp")
    far = replicas // 2
    right = [(i, (i + 1) % replicas) for i in range(replicas)]
    left = [(i, (i - 1) % replicas) for i in range(replicas)]

    def pick(parts, offset):
        return lax.dynamic_index_in_dim(parts, (here + offset + replicas) % replicas, 0, keepdims=False)

    def plus(arrived, parts, offset):
        return (arrived.astype(F32) + pick(parts, offset).astype(F32)).astype(BF)

    sides = [1 if i % 2 == 0 else -1 for i in range(len(chunks))]
    ways = [(right, left) if side == 1 else (left, right) for side in sides]
    long_arm = [pick(parts, far * side) for parts, side in zip(chunks, sides)]
    short_arm = [pick(parts, -(far - 1) * side) for parts, side in zip(chunks, sides)]
    for k in range(far):
        for i, (parts, side, (along, against)) in enumerate(zip(chunks, sides, ways)):
            long_arm[i] = lax.ppermute(long_arm[i], "dp", along)
            if k < far - 1:
                short_arm[i] = lax.ppermute(short_arm[i], "dp", against)
                long_arm[i] = plus(long_arm[i], parts, (far - 1 - k) * side)
                if k < far - 2:
                    short_arm[i] = plus(short_arm[i], parts, -(far - 2 - k) * side)
    return long_arm, short_arm, here


def finish(long_arm, short_arm, chunks, here, gate_mask, up_mask, block, counts):
    each = chunks[0].shape[1]
    blocks_down = gate_mask.shape[0]
    share = each // blocks_down
    total = sum(counts)
    n = len(counts)

    def kernel(where, gm, um, *refs):
        gate_out, up_out = refs[-2], refs[-1]
        at = 0
        for i, count in enumerate(counts):
            for c in range(count):
                both = pl.ds(2 * c * block, 2 * block)
                columns = pl.ds(at * block, block)
                whole = refs[i][:, both].astype(F32) + refs[n + i][:, both].astype(F32)
                whole = whole + refs[2 * n + i][0, :, both].astype(F32)
                for b in range(blocks_down):
                    part = whole[b * share : (b + 1) * share]
                    gate_out[b, :, columns] = (part[:, :block] * gm[b, at].astype(F32)).astype(BF)
                    up_out[b, :, columns] = (part[:, block:] * um[b, at].astype(F32)).astype(BF)
                at += 1

    shape = jax.ShapeDtypeStruct((blocks_down, share, total * block), BF)
    arm = [pl.BlockSpec((each, 2 * block * count), lambda i, w: (0, 0)) for count in counts]
    own = [pl.BlockSpec((1, each, 2 * block * count), lambda i, w: (w[0], 0, 0)) for count in counts]
    whole_out = pl.BlockSpec((blocks_down, share, total * block), lambda i, w: (0, 0, 0))
    return pl.pallas_call(
        kernel,
        grid_spec=pltpu.PrefetchScalarGridSpec(
            num_scalar_prefetch=1,
            grid=(1,),
            in_specs=[in_smem(), in_smem()] + arm + arm + own,
            out_specs=[whole_out, whole_out],
        ),
        out_shape=[shape, shape],
        compiler_params=pltpu.CompilerParams(vmem_limit_bytes=16 * MIB),
        name="finish",
    )(here.astype(jnp.int32).reshape(1), gate_mask, up_mask, *long_arm, *short_arm, *chunks)


def gather_tokens(tokens):
    cols = lax.axis_size("col")
    near = 4
    same_x = [list(range(i, i + near)) for i in range(0, cols, near)]
    along_x = [list(range(i, cols, near)) for i in range(near)]
    tokens = lax.all_gather(tokens, "col", axis=0, tiled=True, axis_index_groups=same_x)
    return lax.all_gather(tokens, "col", axis=0, tiled=True, axis_index_groups=along_x)


def body(tokens, gate_weight, up_weight, gate_mask, up_mask, slope):
    block = gate_weight.shape[0] // gate_mask.shape[0]
    total = gate_mask.shape[1]
    rows = lax.axis_size("row")
    replicas = lax.axis_size("dp")
    cols = lax.axis_size("col")
    counts = (SPLIT, total - SPLIT)
    gathered = gather_tokens(tokens)
    partial, live = forward(gathered, gate_weight, up_weight, gate_mask, up_mask)
    received = lax.all_to_all(partial, "row", 0, 0, tiled=True)
    hidden, slopes = activate(received, slope, block, rows)
    slopes = lax.all_gather(slopes, "row", axis=0, tiled=True)
    chunks = parts_of(gathered, slopes, block, replicas, counts)
    long_arm, short_arm, here = reduce_parts(chunks)
    share = backward(slopes, live)
    pieces = lax.all_to_all(share, "col", 0, 0, tiled=True)
    input_grad = jnp.sum(pieces.reshape((cols, -1) + pieces.shape[1:]), axis=0).astype(BF)
    gate_grad, up_grad = finish(long_arm, short_arm, chunks, here, gate_mask, up_mask, block, counts)
    return hidden, input_grad, gate_grad, up_grad


def solution(mesh):
    return jax.shard_map(
        body,
        mesh=mesh,
        in_specs=(
            P(("dp", "col"), "row"),
            P("row", "col"),
            P("row", "col"),
            P("row", "col"),
            P("row", "col"),
            P(("dp", "row"), "col"),
        ),
        out_specs=(
            P(("dp", "row"), "col"),
            P(("dp", "col"), "row"),
            P("row", "dp", "col"),
            P("row", "dp", "col"),
        ),
        check_vma=False,
    )
```

```python
import jax
import jax.numpy as jnp
from jax import lax
from jax.experimental import pallas as pl
from jax.experimental.pallas import tpu as pltpu
from jax.sharding import PartitionSpec as P

BF = jnp.bfloat16
F32 = jnp.float32
MIB = 1024 * 1024
SPLIT = 4
ROWS = 256


def in_smem():
    return pl.BlockSpec(memory_space=pltpu.SMEM)


def in_vmem():
    return pl.BlockSpec(memory_space=pltpu.VMEM)


def prune(live, gate_w, up_w, gate_mask, up_mask, block, first):
    for b in range(live.shape[0] // block):
        part = pl.ds(b * block, block)
        for j in range(gate_mask.shape[1]):
            one = pl.ds(j * block, block)
            for k, (w, m) in enumerate(((gate_w, gate_mask), (up_w, up_mask))):
                alive = m[first + b, j].astype(F32).astype(BF)
                live[part, pl.ds((2 * j + k) * block, block)] = w[part, one] * alive


def forward(tokens, gate_weight, up_weight, gate_mask, up_mask):
    depth, width = gate_weight.shape
    block = depth // gate_mask.shape[0]
    toks = tokens.shape[0]
    steps = depth // ROWS

    def kernel(gm, um, t, gw, uw, out, live, total):
        step = pl.program_id(0)
        prune(live, gw, uw, gm, um, block, step * (ROWS // block))
        term = jnp.dot(t[...], live[...], preferred_element_type=F32)

        @pl.when(step == 0)
        def _():
            total[...] = term

        @pl.when((step > 0) & (step < steps - 1))
        def _():
            total[...] += term

        @pl.when(step == steps - 1)
        def _():
            out[...] = (total[...] + term).astype(BF)

    return pl.pallas_call(
        kernel,
        grid=(steps,),
        in_specs=[
            in_smem(),
            in_smem(),
            pl.BlockSpec((toks, ROWS), lambda k: (0, k)),
            pl.BlockSpec((ROWS, width), lambda k: (k, 0)),
            pl.BlockSpec((ROWS, width), lambda k: (k, 0)),
        ],
        out_specs=pl.BlockSpec((toks, 2 * width), lambda k: (0, 0)),
        out_shape=jax.ShapeDtypeStruct((toks, 2 * width), BF),
        scratch_shapes=[pltpu.VMEM((ROWS, 2 * width), BF), pltpu.VMEM((toks, 2 * width), F32)],
        cost_estimate=pl.CostEstimate(
            flops=4 * toks * depth * width,
            bytes_accessed=4 * depth * width + 6 * toks * depth,
            transcendentals=0,
        ),
        compiler_params=pltpu.CompilerParams(vmem_limit_bytes=60 * MIB),
        name="forward",
    )(gate_mask, up_mask, tokens, gate_weight, up_weight)


def activate(received, slope, block, sources):
    here, width = slope.shape
    count = width // block

    def kernel(r, s, hidden, slopes):
        for j in range(count):
            both = pl.ds(2 * j * block, 2 * block)
            total = r[pl.ds(0, here), both].astype(F32)
            for k in range(1, sources):
                total = total + r[pl.ds(k * here, here), both].astype(F32)
            gate, up = total[:, :block], total[:, block:]
            sigma = jax.nn.sigmoid(gate)
            act = gate * sigma
            one = pl.ds(j * block, block)
            hidden[:, one] = (act * up).astype(BF)
            wide = s[:, one].astype(F32)
            gate_slope = (wide * up * sigma * (1.0 + gate * (1.0 - sigma))).astype(BF)
            slopes[:, both] = jnp.concatenate([gate_slope, (wide * act).astype(BF)], axis=1)

    return pl.pallas_call(
        kernel,
        in_specs=[in_vmem(), in_vmem()],
        out_specs=[in_vmem(), in_vmem()],
        out_shape=[
            jax.ShapeDtypeStruct((here, width), BF),
            jax.ShapeDtypeStruct((here, 2 * width), BF),
        ],
        cost_estimate=pl.CostEstimate(
            flops=30 * here * width,
            bytes_accessed=here * width * 24,
            transcendentals=here * width,
        ),
        compiler_params=pltpu.CompilerParams(vmem_limit_bytes=12 * MIB),
        name="activate",
    )(received, slope)


def turn(tokens, here, block, replicas):
    toks, depth = tokens.shape
    share = block // replicas
    blocks_down = depth // block

    def kernel(where, t, out, turned):
        turned[...] = t[...].T
        for k in range(replicas):
            owner = lax.rem(where[0] + k, replicas)
            for b in range(blocks_down):
                rows = pl.ds(pl.multiple_of(b * block + owner * share, share), share)
                out[k, pl.ds(b * share, share), :] = turned[rows, :]

    return pl.pallas_call(
        kernel,
        in_specs=[in_smem(), in_vmem()],
        out_specs=in_vmem(),
        out_shape=jax.ShapeDtypeStruct((replicas, blocks_down * share, toks), BF),
        scratch_shapes=[pltpu.VMEM((depth, toks), BF)],
        cost_estimate=pl.CostEstimate(
            flops=0, bytes_accessed=4 * toks * depth, transcendentals=0
        ),
        compiler_params=pltpu.CompilerParams(vmem_limit_bytes=8 * MIB),
        name="turn",
    )(here.reshape(1), tokens)


def parts_of(turned, slopes, wanted, cuts):
    each, toks = turned.shape[1:]

    def kernel(t, s, *outs):
        at = 0
        for k in wanted:
            first = 0
            for width in cuts:
                part = jnp.dot(t[k], s[:, pl.ds(first, width)], preferred_element_type=F32)
                outs[at][...] = part.astype(BF)
                first += width
                at += 1

    return pl.pallas_call(
        kernel,
        in_specs=[in_vmem(), in_vmem()],
        out_specs=[in_vmem()] * (len(wanted) * len(cuts)),
        out_shape=[jax.ShapeDtypeStruct((each, width), BF) for _ in wanted for width in cuts],
        cost_estimate=pl.CostEstimate(
            flops=2 * toks * each * sum(cuts) * len(wanted),
            bytes_accessed=2 * each * sum(cuts) * len(wanted),
            transcendentals=0,
        ),
        compiler_params=pltpu.CompilerParams(vmem_limit_bytes=12 * MIB),
    )(turned, slopes)


def plus(arrived, part, first):
    rows, width = arrived.shape
    whole = part.shape[1]

    def kernel(a, p, out):
        here = pl.ds(first, width)
        out[:, here] = (a[...].astype(F32) + p[:, here].astype(F32)).astype(BF)
        if first:
            out[:, pl.ds(0, first)] = p[:, pl.ds(0, first)]
        if first + width < whole:
            rest = pl.ds(first + width, whole - first - width)
            out[:, rest] = p[:, rest]

    return pl.pallas_call(
        kernel,
        in_specs=[in_vmem(), in_vmem()],
        out_specs=in_vmem(),
        out_shape=jax.ShapeDtypeStruct(part.shape, BF),
        cost_estimate=pl.CostEstimate(
            flops=rows * width, bytes_accessed=6 * rows * whole, transcendentals=0
        ),
        compiler_params=pltpu.CompilerParams(vmem_limit_bytes=6 * MIB),
    )(arrived, part)


def backward(slopes, gate_weight, up_weight, gate_mask, up_mask):
    depth, width = gate_weight.shape
    block = depth // gate_mask.shape[0]
    toks = slopes.shape[0]

    def kernel(gm, um, s, gw, uw, out, live):
        prune(live, gw, uw, gm, um, block, pl.program_id(0) * (ROWS // block))
        out[...] = lax.dot_general(
            s[...], live[...], (((1,), (1,)), ((), ())), preferred_element_type=F32
        )

    return pl.pallas_call(
        kernel,
        grid=(depth // ROWS,),
        in_specs=[
            in_smem(),
            in_smem(),
            pl.BlockSpec((toks, 2 * width), lambda k: (0, 0)),
            pl.BlockSpec((ROWS, width), lambda k: (k, 0)),
            pl.BlockSpec((ROWS, width), lambda k: (k, 0)),
        ],
        out_specs=pl.BlockSpec((toks, ROWS), lambda k: (0, k)),
        out_shape=jax.ShapeDtypeStruct((toks, depth), F32),
        scratch_shapes=[pltpu.VMEM((ROWS, 2 * width), BF)],
        cost_estimate=pl.CostEstimate(
            flops=4 * toks * depth * width,
            bytes_accessed=4 * depth * width + 6 * toks * depth,
            transcendentals=0,
        ),
        compiler_params=pltpu.CompilerParams(vmem_limit_bytes=20 * MIB),
        name="backward",
    )(gate_mask, up_mask, slopes, gate_weight, up_weight)


def reduce_parts(turned, slopes, cut, weights):
    replicas = lax.axis_size("dp")
    far = replicas // 2
    width = slopes.shape[1]
    right = [(i, (i + 1) % replicas) for i in range(replicas)]
    left = [(i, (i - 1) % replicas) for i in range(replicas)]
    to_right, to_left = parts_of(turned, slopes, [far], [cut, width - cut])
    near = [k for i in range(far - 1, 0, -1) for k in (i, replicas - i)] + [0]
    parts = dict(zip(near, parts_of(turned, slopes, near, [width])))
    share = backward(slopes, *weights)
    for k in range(far - 1, -1, -1):
        from_left = lax.ppermute(to_right, "dp", right)
        from_right = lax.ppermute(to_left, "dp", left)
        if k:
            to_right = plus(from_left, parts[k], 0)
            to_left = plus(from_right, parts[replicas - k], cut if k == far - 1 else 0)
    return (from_left, from_right, parts[0]), share


def finish(sums, gate_mask, up_mask, block):
    each, _ = sums[0].shape
    blocks_down, total = gate_mask.shape
    share = each // blocks_down

    def kernel(gm, um, *refs):
        gate_out, up_out = refs[-2], refs[-1]
        for c in range(total):
            both = pl.ds(2 * c * block, 2 * block)
            columns = pl.ds(c * block, block)
            whole = refs[0][:, both].astype(F32)
            for r in refs[1:-2]:
                whole = whole + r[:, both].astype(F32)
            for b in range(blocks_down):
                part = whole[b * share : (b + 1) * share]
                gate_out[b, :, columns] = (part[:, :block] * gm[b, c].astype(F32)).astype(BF)
                up_out[b, :, columns] = (part[:, block:] * um[b, c].astype(F32)).astype(BF)

    shape = jax.ShapeDtypeStruct((blocks_down, share, total * block), BF)
    return pl.pallas_call(
        kernel,
        in_specs=[in_smem(), in_smem()] + [in_vmem()] * len(sums),
        out_specs=[in_vmem(), in_vmem()],
        out_shape=[shape, shape],
        compiler_params=pltpu.CompilerParams(vmem_limit_bytes=8 * MIB),
        name="finish",
    )(gate_mask, up_mask, *sums)


def gather_tokens(tokens):
    cols = lax.axis_size("col")
    near = 4
    same_x = [list(range(i, i + near)) for i in range(0, cols, near)]
    along_x = [list(range(i, cols, near)) for i in range(near)]
    tokens = lax.all_gather(tokens, "col", axis=0, tiled=True, axis_index_groups=same_x)
    return lax.all_gather(tokens, "col", axis=0, tiled=True, axis_index_groups=along_x)


def body(tokens, gate_weight, up_weight, gate_mask, up_mask, slope):
    block = gate_weight.shape[0] // gate_mask.shape[0]
    rows = lax.axis_size("row")
    replicas = lax.axis_size("dp")
    cols = lax.axis_size("col")
    weights = (gate_weight, up_weight, gate_mask, up_mask)
    here = lax.axis_index("dp").astype(jnp.int32)
    return layer(tokens, weights, slope, block, rows, replicas, cols, here)


def layer(tokens, weights, slope, block, rows, replicas, cols, here):
    gathered = gather_tokens(tokens)
    partial = forward(gathered, *weights)
    received = lax.all_to_all(partial, "row", 0, 0, tiled=True)
    turned = turn(gathered, here, block, replicas)
    hidden, slopes = activate(received, slope, block, rows)
    slopes = lax.all_gather(slopes, "row", axis=0, tiled=True)
    sums, share = reduce_parts(turned, slopes, 2 * block * SPLIT, weights)
    pieces = lax.all_to_all(share, "col", 0, 0, tiled=True)
    input_grad = jnp.sum(pieces.reshape((cols, -1) + pieces.shape[1:]), axis=0).astype(BF)
    gate_grad, up_grad = finish(sums, weights[2], weights[3], block)
    return hidden, input_grad, gate_grad, up_grad


def solution(mesh):
    return jax.shard_map(
        body,
        mesh=mesh,
        in_specs=(
            P(("dp", "col"), "row"),
            P("row", "col"),
            P("row", "col"),
            P("row", "col"),
            P("row", "col"),
            P(("dp", "row"), "col"),
        ),
        out_specs=(
            P(("dp", "row"), "col"),
            P(("dp", "col"), "row"),
            P("row", "dp", "col"),
            P("row", "dp", "col"),
        ),
        check_vma=False,
    )
```

```python
import jax
import jax.numpy as jnp
from jax import lax
from jax.experimental import pallas as pl
from jax.experimental.pallas import tpu as pltpu
from jax.sharding import PartitionSpec as P

BF = jnp.bfloat16
F32 = jnp.float32
MIB = 1024 * 1024
ROWS = 256


def in_smem():
    return pl.BlockSpec(memory_space=pltpu.SMEM)


def in_vmem():
    return pl.BlockSpec(memory_space=pltpu.VMEM)


def prune(live, gate_w, up_w, gate_mask, up_mask, block, first):
    for b in range(live.shape[0] // block):
        part = pl.ds(b * block, block)
        for j in range(gate_mask.shape[1]):
            one = pl.ds(j * block, block)
            for k, (w, m) in enumerate(((gate_w, gate_mask), (up_w, up_mask))):
                alive = m[first + b, j].astype(F32).astype(BF)
                live[part, pl.ds((2 * j + k) * block, block)] = w[part, one] * alive


def forward(tokens, gate_weight, up_weight, gate_mask, up_mask):
    depth, width = gate_weight.shape
    block = depth // gate_mask.shape[0]
    toks = tokens.shape[0]
    steps = depth // ROWS

    def kernel(gm, um, t, gw, uw, out, live, total):
        step = pl.program_id(0)
        prune(live, gw, uw, gm, um, block, step * (ROWS // block))
        term = jnp.dot(t[...], live[...], preferred_element_type=F32)

        @pl.when(step == 0)
        def _():
            total[...] = term

        @pl.when((step > 0) & (step < steps - 1))
        def _():
            total[...] += term

        @pl.when(step == steps - 1)
        def _():
            out[...] = (total[...] + term).astype(BF)

    return pl.pallas_call(
        kernel,
        grid=(steps,),
        in_specs=[
            in_smem(),
            in_smem(),
            pl.BlockSpec((toks, ROWS), lambda k: (0, k)),
            pl.BlockSpec((ROWS, width), lambda k: (k, 0)),
            pl.BlockSpec((ROWS, width), lambda k: (k, 0)),
        ],
        out_specs=pl.BlockSpec((toks, 2 * width), lambda k: (0, 0)),
        out_shape=jax.ShapeDtypeStruct((toks, 2 * width), BF),
        scratch_shapes=[pltpu.VMEM((ROWS, 2 * width), BF), pltpu.VMEM((toks, 2 * width), F32)],
        cost_estimate=pl.CostEstimate(
            flops=4 * toks * depth * width,
            bytes_accessed=4 * depth * width + 6 * toks * depth,
            transcendentals=0,
        ),
        compiler_params=pltpu.CompilerParams(vmem_limit_bytes=60 * MIB),
        name="forward",
    )(gate_mask, up_mask, tokens, gate_weight, up_weight)


def activate(received, slope, block, sources):
    here, width = slope.shape
    count = width // block

    def kernel(r, s, hidden, slopes):
        for j in range(count):
            both = pl.ds(2 * j * block, 2 * block)
            total = r[pl.ds(0, here), both].astype(F32)
            for k in range(1, sources):
                total = total + r[pl.ds(k * here, here), both].astype(F32)
            gate, up = total[:, :block], total[:, block:]
            sigma = jax.nn.sigmoid(gate)
            act = gate * sigma
            one = pl.ds(j * block, block)
            hidden[:, one] = (act * up).astype(BF)
            wide = s[:, one].astype(F32)
            gate_slope = (wide * up * sigma * (1.0 + gate * (1.0 - sigma))).astype(BF)
            slopes[:, both] = jnp.concatenate([gate_slope, (wide * act).astype(BF)], axis=1)

    return pl.pallas_call(
        kernel,
        in_specs=[in_vmem(), in_vmem()],
        out_specs=[in_vmem(), in_vmem()],
        out_shape=[
            jax.ShapeDtypeStruct((here, width), BF),
            jax.ShapeDtypeStruct((here, 2 * width), BF),
        ],
        cost_estimate=pl.CostEstimate(
            flops=30 * here * width,
            bytes_accessed=here * width * 24,
            transcendentals=here * width,
        ),
        compiler_params=pltpu.CompilerParams(vmem_limit_bytes=12 * MIB),
        name="activate",
    )(received, slope)


def turn(tokens, here, way, block, replicas, reach):
    toks, depth = tokens.shape
    share = block // replicas
    blocks_down = depth // block

    def kernel(place, t, out, turned):
        turned[...] = t[...].T
        for k in range(reach):
            owner = lax.rem(place[0] + place[1] * k + replicas, replicas)
            for b in range(blocks_down):
                rows = pl.ds(pl.multiple_of(b * block + owner * share, share), share)
                out[k, pl.ds(b * share, share), :] = turned[rows, :]

    return pl.pallas_call(
        kernel,
        in_specs=[in_smem(), in_vmem()],
        out_specs=in_vmem(),
        out_shape=jax.ShapeDtypeStruct((reach, blocks_down * share, toks), BF),
        scratch_shapes=[pltpu.VMEM((depth, toks), BF)],
        cost_estimate=pl.CostEstimate(
            flops=0, bytes_accessed=4 * toks * depth, transcendentals=0
        ),
        compiler_params=pltpu.CompilerParams(vmem_limit_bytes=8 * MIB),
        name="turn",
    )(jnp.stack([here, way]), tokens)


def parts_of(turned, slopes, wanted):
    each, toks = turned.shape[1:]
    width = slopes.shape[1]

    def kernel(t, s, *outs):
        for k, out in zip(wanted, outs):
            out[...] = jnp.dot(t[k], s[...], preferred_element_type=F32).astype(BF)

    return pl.pallas_call(
        kernel,
        in_specs=[in_vmem(), in_vmem()],
        out_specs=[in_vmem()] * len(wanted),
        out_shape=[jax.ShapeDtypeStruct((each, width), BF) for _ in wanted],
        cost_estimate=pl.CostEstimate(
            flops=2 * toks * each * width * len(wanted),
            bytes_accessed=2 * each * width * len(wanted),
            transcendentals=0,
        ),
        compiler_params=pltpu.CompilerParams(vmem_limit_bytes=10 * MIB),
    )(turned, slopes)


def plus(arrived, part):
    def kernel(a, p, out):
        out[...] = (a[...].astype(F32) + p[...].astype(F32)).astype(BF)

    size = part.shape[0] * part.shape[1]
    return pl.pallas_call(
        kernel,
        in_specs=[in_vmem(), in_vmem()],
        out_specs=in_vmem(),
        out_shape=jax.ShapeDtypeStruct(part.shape, BF),
        cost_estimate=pl.CostEstimate(flops=size, bytes_accessed=6 * size, transcendentals=0),
        compiler_params=pltpu.CompilerParams(vmem_limit_bytes=6 * MIB),
        name="plus",
    )(arrived, part)


def backward(slopes, gate_weight, up_weight, gate_mask, up_mask):
    depth, width = gate_weight.shape
    block = depth // gate_mask.shape[0]
    toks = slopes.shape[0]

    def kernel(gm, um, s, gw, uw, out, live):
        prune(live, gw, uw, gm, um, block, pl.program_id(0) * (ROWS // block))
        out[...] = lax.dot_general(
            s[...], live[...], (((1,), (1,)), ((), ())), preferred_element_type=F32
        )

    return pl.pallas_call(
        kernel,
        grid=(depth // ROWS,),
        in_specs=[
            in_smem(),
            in_smem(),
            pl.BlockSpec((toks, 2 * width), lambda k: (0, 0)),
            pl.BlockSpec((ROWS, width), lambda k: (k, 0)),
            pl.BlockSpec((ROWS, width), lambda k: (k, 0)),
        ],
        out_specs=pl.BlockSpec((toks, ROWS), lambda k: (0, k)),
        out_shape=jax.ShapeDtypeStruct((toks, depth), F32),
        scratch_shapes=[pltpu.VMEM((ROWS, 2 * width), BF)],
        cost_estimate=pl.CostEstimate(
            flops=4 * toks * depth * width,
            bytes_accessed=4 * depth * width + 6 * toks * depth,
            transcendentals=0,
        ),
        compiler_params=pltpu.CompilerParams(vmem_limit_bytes=20 * MIB),
        name="backward",
    )(gate_mask, up_mask, slopes, gate_weight, up_weight)


def reduce_parts(turned, slopes, weights):
    replicas = lax.axis_size("dp")
    cols = lax.axis_size("col")
    far = replicas // 2
    ring = [
        (p * cols + c, (p + 1 - 2 * (c % 2)) % replicas * cols + c)
        for p in range(replicas)
        for c in range(cols)
    ]
    swap = [(c, c ^ 1) for c in range(cols)]
    own = parts_of(turned, slopes, [far])[0]
    other_slopes = lax.ppermute(slopes, "col", swap)
    near = list(range(far - 1, 0, -1))
    own_parts = parts_of(turned, slopes, near + [0])
    share = backward(slopes, *weights)
    other_parts = parts_of(turned, other_slopes, near)
    other = other_parts[0]
    for hop in range(far):
        own = lax.ppermute(own, ("dp", "col"), ring)
        if hop < far - 1:
            own = plus(own, own_parts[hop])
            other = lax.ppermute(other, ("dp", "col"), ring)
            if hop < far - 2:
                other = plus(other, other_parts[hop + 1])
    other = lax.ppermute(other, "col", swap)
    return (own, other, own_parts[far - 1]), share


def finish(sums, gate_mask, up_mask, block):
    each, _ = sums[0].shape
    blocks_down, total = gate_mask.shape
    share = each // blocks_down

    def kernel(gm, um, *refs):
        gate_out, up_out = refs[-2], refs[-1]
        for c in range(total):
            both = pl.ds(2 * c * block, 2 * block)
            columns = pl.ds(c * block, block)
            whole = refs[0][:, both].astype(F32)
            for r in refs[1:-2]:
                whole = whole + r[:, both].astype(F32)
            for b in range(blocks_down):
                part = whole[b * share : (b + 1) * share]
                gate_out[b, :, columns] = (part[:, :block] * gm[b, c].astype(F32)).astype(BF)
                up_out[b, :, columns] = (part[:, block:] * um[b, c].astype(F32)).astype(BF)

    shape = jax.ShapeDtypeStruct((blocks_down, share, total * block), BF)
    return pl.pallas_call(
        kernel,
        in_specs=[in_smem(), in_smem()] + [in_vmem()] * len(sums),
        out_specs=[in_vmem(), in_vmem()],
        out_shape=[shape, shape],
        compiler_params=pltpu.CompilerParams(vmem_limit_bytes=8 * MIB),
        name="finish",
    )(gate_mask, up_mask, *sums)


def gather_tokens(tokens):
    cols = lax.axis_size("col")
    near = 4
    same_x = [list(range(i, i + near)) for i in range(0, cols, near)]
    along_x = [list(range(i, cols, near)) for i in range(near)]
    tokens = lax.all_gather(tokens, "col", axis=0, tiled=True, axis_index_groups=same_x)
    return lax.all_gather(tokens, "col", axis=0, tiled=True, axis_index_groups=along_x)


def body(tokens, gate_weight, up_weight, gate_mask, up_mask, slope):
    block = gate_weight.shape[0] // gate_mask.shape[0]
    rows = lax.axis_size("row")
    replicas = lax.axis_size("dp")
    cols = lax.axis_size("col")
    weights = (gate_weight, up_weight, gate_mask, up_mask)
    here = lax.axis_index("dp").astype(jnp.int32)
    way = 1 - 2 * (lax.axis_index("col").astype(jnp.int32) % 2)
    return layer(tokens, weights, slope, block, rows, replicas, cols, here, way)


def layer(tokens, weights, slope, block, rows, replicas, cols, here, way):
    gathered = gather_tokens(tokens)
    partial = forward(gathered, *weights)
    received = lax.all_to_all(partial, "row", 0, 0, tiled=True)
    turned = turn(gathered, here, way, block, replicas, replicas // 2 + 1)
    hidden, slopes = activate(received, slope, block, rows)
    slopes = lax.all_gather(slopes, "row", axis=0, tiled=True)
    sums, share = reduce_parts(turned, slopes, weights)
    pieces = lax.all_to_all(share, "col", 0, 0, tiled=True)
    input_grad = jnp.sum(pieces.reshape((cols, -1) + pieces.shape[1:]), axis=0).astype(BF)
    gate_grad, up_grad = finish(sums, weights[2], weights[3], block)
    return hidden, input_grad, gate_grad, up_grad


def solution(mesh):
    return jax.shard_map(
        body,
        mesh=mesh,
        in_specs=(
            P(("dp", "col"), "row"),
            P("row", "col"),
            P("row", "col"),
            P("row", "col"),
            P("row", "col"),
            P(("dp", "row"), "col"),
        ),
        out_specs=(
            P(("dp", "row"), "col"),
            P(("dp", "col"), "row"),
            P("row", "dp", "col"),
            P("row", "dp", "col"),
        ),
        check_vma=False,
    )
```

```python
import jax
import jax.numpy as jnp
from jax import lax
from jax.experimental import pallas as pl
from jax.experimental.pallas import tpu as pltpu
from jax.sharding import PartitionSpec as P

BF = jnp.bfloat16
F32 = jnp.float32
MIB = 1024 * 1024
ROWS = 256


def in_smem():
    return pl.BlockSpec(memory_space=pltpu.SMEM)


def in_vmem():
    return pl.BlockSpec(memory_space=pltpu.VMEM)


def prune(live, gate_w, up_w, gate_mask, up_mask, block, first):
    for b in range(live.shape[0] // block):
        part = pl.ds(b * block, block)
        for j in range(gate_mask.shape[1]):
            one = pl.ds(j * block, block)
            for k, (w, m) in enumerate(((gate_w, gate_mask), (up_w, up_mask))):
                alive = m[first + b, j].astype(F32).astype(BF)
                live[part, pl.ds((2 * j + k) * block, block)] = w[part, one] * alive


def forward(tokens, gate_weight, up_weight, gate_mask, up_mask):
    depth, width = gate_weight.shape
    block = depth // gate_mask.shape[0]
    toks = tokens.shape[0]
    steps = depth // ROWS

    def kernel(gm, um, t, gw, uw, out, live, total):
        step = pl.program_id(0)
        prune(live, gw, uw, gm, um, block, step * (ROWS // block))
        term = jnp.dot(t[...], live[...], preferred_element_type=F32)

        @pl.when(step == 0)
        def _():
            total[...] = term

        @pl.when((step > 0) & (step < steps - 1))
        def _():
            total[...] += term

        @pl.when(step == steps - 1)
        def _():
            out[...] = (total[...] + term).astype(BF)

    return pl.pallas_call(
        kernel,
        grid=(steps,),
        in_specs=[
            in_smem(),
            in_smem(),
            pl.BlockSpec((toks, ROWS), lambda k: (0, k)),
            pl.BlockSpec((ROWS, width), lambda k: (k, 0)),
            pl.BlockSpec((ROWS, width), lambda k: (k, 0)),
        ],
        out_specs=pl.BlockSpec((toks, 2 * width), lambda k: (0, 0)),
        out_shape=jax.ShapeDtypeStruct((toks, 2 * width), BF),
        scratch_shapes=[pltpu.VMEM((ROWS, 2 * width), BF), pltpu.VMEM((toks, 2 * width), F32)],
        cost_estimate=pl.CostEstimate(
            flops=4 * toks * depth * width,
            bytes_accessed=4 * depth * width + 6 * toks * depth,
            transcendentals=0,
        ),
        compiler_params=pltpu.CompilerParams(vmem_limit_bytes=60 * MIB),
        name="forward",
    )(gate_mask, up_mask, tokens, gate_weight, up_weight)


def activate(received, slope, block, sources):
    here, width = slope.shape
    count = width // block

    def kernel(r, s, hidden, slopes):
        for j in range(count):
            both = pl.ds(2 * j * block, 2 * block)
            total = r[pl.ds(0, here), both].astype(F32)
            for k in range(1, sources):
                total = total + r[pl.ds(k * here, here), both].astype(F32)
            gate, up = total[:, :block], total[:, block:]
            sigma = jax.nn.sigmoid(gate)
            act = gate * sigma
            one = pl.ds(j * block, block)
            hidden[:, one] = (act * up).astype(BF)
            wide = s[:, one].astype(F32)
            gate_slope = (wide * up * sigma * (1.0 + gate * (1.0 - sigma))).astype(BF)
            slopes[:, both] = jnp.concatenate([gate_slope, (wide * act).astype(BF)], axis=1)

    return pl.pallas_call(
        kernel,
        in_specs=[in_vmem(), in_vmem()],
        out_specs=[in_vmem(), in_vmem()],
        out_shape=[
            jax.ShapeDtypeStruct((here, width), BF),
            jax.ShapeDtypeStruct((here, 2 * width), BF),
        ],
        cost_estimate=pl.CostEstimate(
            flops=30 * here * width,
            bytes_accessed=here * width * 24,
            transcendentals=here * width,
        ),
        compiler_params=pltpu.CompilerParams(vmem_limit_bytes=12 * MIB),
        name="activate",
    )(received, slope)


def turn(tokens, here, way, block, replicas, reach):
    toks, depth = tokens.shape
    share = block // replicas
    blocks_down = depth // block

    def kernel(place, t, out, turned):
        turned[...] = t[...].T
        for k in range(reach):
            owner = lax.rem(place[0] + place[1] * k + replicas, replicas)
            for b in range(blocks_down):
                rows = pl.ds(pl.multiple_of(b * block + owner * share, share), share)
                out[k, pl.ds(b * share, share), :] = turned[rows, :]

    return pl.pallas_call(
        kernel,
        in_specs=[in_smem(), in_vmem()],
        out_specs=in_vmem(),
        out_shape=jax.ShapeDtypeStruct((reach, blocks_down * share, toks), BF),
        scratch_shapes=[pltpu.VMEM((depth, toks), BF)],
        cost_estimate=pl.CostEstimate(
            flops=0, bytes_accessed=4 * toks * depth, transcendentals=0
        ),
        compiler_params=pltpu.CompilerParams(vmem_limit_bytes=8 * MIB),
        name="turn",
    )(jnp.stack([here, way]), tokens)


def parts_of(turned, slopes, wanted):
    each, toks = turned.shape[1:]
    width = slopes.shape[1]

    def kernel(t, s, *outs):
        for k, out in zip(wanted, outs):
            out[...] = jnp.dot(t[k], s[...], preferred_element_type=F32).astype(BF)

    return pl.pallas_call(
        kernel,
        in_specs=[in_vmem(), in_vmem()],
        out_specs=[in_vmem()] * len(wanted),
        out_shape=[jax.ShapeDtypeStruct((each, width), BF) for _ in wanted],
        cost_estimate=pl.CostEstimate(
            flops=2 * toks * each * width * len(wanted),
            bytes_accessed=2 * each * width * len(wanted),
            transcendentals=0,
        ),
        compiler_params=pltpu.CompilerParams(vmem_limit_bytes=10 * MIB),
    )(turned, slopes)


def plus(arrived, part):
    def kernel(a, p, out):
        out[...] = (a[...].astype(F32) + p[...].astype(F32)).astype(BF)

    size = part.shape[0] * part.shape[1]
    return pl.pallas_call(
        kernel,
        in_specs=[in_vmem(), in_vmem()],
        out_specs=in_vmem(),
        out_shape=jax.ShapeDtypeStruct(part.shape, BF),
        cost_estimate=pl.CostEstimate(flops=size, bytes_accessed=6 * size, transcendentals=0),
        compiler_params=pltpu.CompilerParams(vmem_limit_bytes=6 * MIB),
        name="plus",
    )(arrived, part)


def backward(slopes, gate_weight, up_weight, gate_mask, up_mask):
    depth, width = gate_weight.shape
    block = depth // gate_mask.shape[0]
    toks = slopes.shape[0]

    def kernel(gm, um, s, gw, uw, out, live):
        prune(live, gw, uw, gm, um, block, pl.program_id(0) * (ROWS // block))
        out[...] = lax.dot_general(
            s[...], live[...], (((1,), (1,)), ((), ())), preferred_element_type=F32
        ).astype(BF)

    return pl.pallas_call(
        kernel,
        grid=(depth // ROWS,),
        in_specs=[
            in_smem(),
            in_smem(),
            pl.BlockSpec((toks, 2 * width), lambda k: (0, 0)),
            pl.BlockSpec((ROWS, width), lambda k: (k, 0)),
            pl.BlockSpec((ROWS, width), lambda k: (k, 0)),
        ],
        out_specs=pl.BlockSpec((toks, ROWS), lambda k: (0, k)),
        out_shape=jax.ShapeDtypeStruct((toks, depth), BF),
        scratch_shapes=[pltpu.VMEM((ROWS, 2 * width), BF)],
        cost_estimate=pl.CostEstimate(
            flops=4 * toks * depth * width,
            bytes_accessed=4 * depth * width + 6 * toks * depth,
            transcendentals=0,
        ),
        compiler_params=pltpu.CompilerParams(vmem_limit_bytes=20 * MIB),
        name="backward",
    )(gate_mask, up_mask, slopes, gate_weight, up_weight)


def reduce_parts(turned, slopes, weights):
    replicas = lax.axis_size("dp")
    cols = lax.axis_size("col")
    far = replicas // 2
    ring = [
        (p * cols + c, (p + 1 - 2 * (c % 2)) % replicas * cols + c)
        for p in range(replicas)
        for c in range(cols)
    ]
    swap = [(c, c ^ 1) for c in range(cols)]
    own = parts_of(turned, slopes, [far])[0]
    other_slopes = lax.ppermute(slopes, "col", swap)
    near = list(range(far - 1, 0, -1))
    own_parts = parts_of(turned, slopes, near + [0])
    share = backward(slopes, *weights)
    other_parts = parts_of(turned, other_slopes, near)
    other = other_parts[0]
    for hop in range(far):
        own = lax.ppermute(own, ("dp", "col"), ring)
        if hop < far - 1:
            own = plus(own, own_parts[hop])
            other = lax.ppermute(other, ("dp", "col"), ring)
            if hop < far - 2:
                other = plus(other, other_parts[hop + 1])
    other = lax.ppermute(other, "col", swap)
    return (own, other, own_parts[far - 1]), share


def finish(sums, gate_mask, up_mask, block):
    each, _ = sums[0].shape
    blocks_down, total = gate_mask.shape
    share = each // blocks_down

    def kernel(gm, um, *refs):
        gate_out, up_out = refs[-2], refs[-1]
        for c in range(total):
            both = pl.ds(2 * c * block, 2 * block)
            columns = pl.ds(c * block, block)
            whole = refs[0][:, both].astype(F32)
            for r in refs[1:-2]:
                whole = whole + r[:, both].astype(F32)
            for b in range(blocks_down):
                part = whole[b * share : (b + 1) * share]
                gate_out[b, :, columns] = (part[:, :block] * gm[b, c].astype(F32)).astype(BF)
                up_out[b, :, columns] = (part[:, block:] * um[b, c].astype(F32)).astype(BF)

    shape = jax.ShapeDtypeStruct((blocks_down, share, total * block), BF)
    return pl.pallas_call(
        kernel,
        in_specs=[in_smem(), in_smem()] + [in_vmem()] * len(sums),
        out_specs=[in_vmem(), in_vmem()],
        out_shape=[shape, shape],
        compiler_params=pltpu.CompilerParams(vmem_limit_bytes=8 * MIB),
        name="finish",
    )(gate_mask, up_mask, *sums)


def gather_tokens(tokens):
    cols = lax.axis_size("col")
    near = 4
    same_x = [list(range(i, i + near)) for i in range(0, cols, near)]
    along_x = [list(range(i, cols, near)) for i in range(near)]
    tokens = lax.all_gather(tokens, "col", axis=0, tiled=True, axis_index_groups=same_x)
    return lax.all_gather(tokens, "col", axis=0, tiled=True, axis_index_groups=along_x)


def body(tokens, gate_weight, up_weight, gate_mask, up_mask, slope):
    block = gate_weight.shape[0] // gate_mask.shape[0]
    rows = lax.axis_size("row")
    replicas = lax.axis_size("dp")
    cols = lax.axis_size("col")
    weights = (gate_weight, up_weight, gate_mask, up_mask)
    here = lax.axis_index("dp").astype(jnp.int32)
    way = 1 - 2 * (lax.axis_index("col").astype(jnp.int32) % 2)
    return layer(tokens, weights, slope, block, rows, replicas, cols, here, way)


def layer(tokens, weights, slope, block, rows, replicas, cols, here, way):
    gathered = gather_tokens(tokens)
    partial = forward(gathered, *weights)
    received = lax.all_to_all(partial, "row", 0, 0, tiled=True)
    turned = turn(gathered, here, way, block, replicas, replicas // 2 + 1)
    hidden, slopes = activate(received, slope, block, rows)
    slopes = lax.all_gather(slopes, "row", axis=0, tiled=True)
    sums, share = reduce_parts(turned, slopes, weights)
    pieces = lax.all_to_all(share, "col", 0, 0, tiled=True)
    pieces = pieces.reshape((cols, -1) + pieces.shape[1:])
    input_grad = jnp.sum(pieces.astype(F32), axis=0).astype(BF)
    gate_grad, up_grad = finish(sums, weights[2], weights[3], block)
    return hidden, input_grad, gate_grad, up_grad


def solution(mesh):
    return jax.shard_map(
        body,
        mesh=mesh,
        in_specs=(
            P(("dp", "col"), "row"),
            P("row", "col"),
            P("row", "col"),
            P("row", "col"),
            P("row", "col"),
            P(("dp", "row"), "col"),
        ),
        out_specs=(
            P(("dp", "row"), "col"),
            P(("dp", "col"), "row"),
            P("row", "dp", "col"),
            P("row", "dp", "col"),
        ),
        check_vma=False,
    )
```
